32 devices in a mesh: row: 16 (over z, y, x), col: 2 (over core).
Axes of the slice: x: 2, y: 2, z: 4, core: 2. Of those that a mesh axis runs over, the one named last changes fastest.
Arguments:
- ancestor: float32 [16384, 16384], P('row', 'col'), may hold values from -4 to 4, as said below
- panels: float32 [4, 4096, 256], P(None, 'row'), may hold values from -0.125 to 0.125
- tile_lists: int32 [4, 16], replicated, may hold values from -1 to 63, as said below
- diag_inverse: float32 [4, 256, 256], replicated, may hold values from -3 to 3
Outputs:
- off_blocks: float32 [4, 16384, 256], P(None, ('row', 'col'))
- diag_blocks: float32 [4, 256, 256], replicated
The draws below stay inside these ranges and needn't reach their ends.
Inputs may be any that keep to these rules, and one draw needn't show every extreme that they name: `ancestor`: symmetric. `tile_lists`: row k holds count_k distinct row blocks in ascending order followed by -1 in the remaining slots; count_k lies between 8 and 16, and some row holds exactly 16. Every row lists row block 0 and row block 32.
All inputs are finite; a program needn't handle non-finite values.
Results may differ from the reference program's by a relative error of at most 0.00011.
Values sent between devices are 32-bit elements; how exact they have to be, the bound alone decides.
No kernel may reach another device: no remote copies, remote signals or barrier semaphores. Data moves between devices by JAX's collectives and lax.ppermute only.
A program may use at most 128 MiB of HBM per device.

```python
import jax
import jax.numpy as jnp
from jax import lax

ORDER = 16384
WIDTH = 256
TILE = 256
SLOTS = 16
SUPERNODES = 4


def draw_ancestor(key, part):
    base = jax.random.normal(jax.random.fold_in(key, 11), (ORDER, ORDER), jnp.float32)
    sym = (base + base.T) * 0.5 ** 0.5 * 0.5
    return jnp.clip(sym, -4.0, 4.0)


def draw_tile_lists(key, part):
    tiles_all = ORDER // TILE
    middle = tiles_all // 2
    every_tile = jnp.arange(tiles_all, dtype=jnp.int32)
    counts = jax.random.randint(jax.random.fold_in(key, 21), (SUPERNODES,), SLOTS // 2, SLOTS + 1)
    fullest = jax.random.randint(jax.random.fold_in(key, 22), (), 0, SUPERNODES)
    counts = jnp.where(jnp.arange(SUPERNODES) == fullest, SLOTS, counts)
    slots_at = jnp.arange(SLOTS, dtype=jnp.int32)
    rows_out = []
    for supernode in range(SUPERNODES):
        shuffled = jax.random.permutation(jax.random.fold_in(key, 100 + supernode), tiles_all).astype(jnp.int32)
        ranks = jnp.argsort(shuffled).astype(jnp.int32)
        forced = (every_tile == 0) | (every_tile == middle)
        ranks = jnp.where(forced, -1, ranks).astype(jnp.int32)
        order_tiles = jnp.argsort(ranks, stable=True).astype(jnp.int32)[:SLOTS]
        kept = jnp.where(slots_at < counts[supernode], order_tiles, tiles_all)
        kept = jnp.sort(kept)
        rows_out.append(jnp.where(kept >= tiles_all, -1, kept).astype(jnp.int32))
    return jnp.stack(rows_out).astype(jnp.int32)


def block_levels(rng, shape, pieces, least, top_value):
    loudness, own = 1.0, jax.random.fold_in(rng, 6)
    for axis_at, shards_of in pieces:
        heights = jnp.exp(jax.random.uniform(jax.random.fold_in(own, axis_at), (shards_of,), jnp.float32, least / len(pieces), top_value / len(pieces)))
        loudness = loudness * jnp.repeat(heights, shape[axis_at] // shards_of).reshape([-1 if axis == axis_at else 1 for axis in range(len(shape))])
    return loudness


def scatter_about(own_key, extent, deviation, most, split=(), held_as=jnp.bfloat16):
    factor_of = block_levels(own_key, extent, split, -0.22, 0.18) if split else 1.0
    result = jax.random.normal(own_key, extent, jnp.float32) * deviation * factor_of
    return jnp.minimum(jnp.maximum(result, -most), most).astype(held_as)


def setup_inputs(seed: int = 0) -> dict:
    streams_of = jax.random.split(jax.random.key(seed), 5)
    return {
        "ancestor": draw_ancestor(jax.random.fold_in(streams_of[4], 71), 0),
        "panels": scatter_about(streams_of[1], (SUPERNODES, SLOTS * TILE, WIDTH), (2.0 / (SLOTS * TILE) ** 0.5), 0.125, ((1, 16),), jnp.float32),
        "tile_lists": draw_tile_lists(jax.random.fold_in(streams_of[4], 71), 0),
        "diag_inverse": scatter_about(streams_of[3], (SUPERNODES, WIDTH, WIDTH), 0.5, 3.0, (), jnp.float32),
    }


def reference(ancestor, panels, tile_lists, diag_inverse):
    tiles_all = ORDER // TILE
    positions = jnp.arange(tiles_all, dtype=jnp.int32)
    off_pieces = []
    diag_pieces = []
    for supernode in range(SUPERNODES):
        listed = tile_lists[supernode].astype(jnp.int32)
        present = listed >= 0
        safe_ids = jnp.where(present, listed, 0).astype(jnp.int32)
        panel = panels[supernode].reshape(SLOTS, TILE, WIDTH) * present[:, None, None].astype(jnp.float32)
        columns = jnp.take(ancestor.reshape(ORDER, tiles_all, TILE), safe_ids, axis=1)
        product = jnp.einsum("nst,stw->nw", columns, panel, precision=lax.Precision.HIGHEST)
        listed_rows = jnp.any(positions[:, None] == listed[None, :], axis=1)
        row_valid = jnp.repeat(listed_rows, TILE).astype(jnp.float32)
        off_pieces.append(-(row_valid[:, None] * product))
        chosen = jnp.take(product.reshape(tiles_all, TILE, WIDTH), safe_ids, axis=0)
        extra = jnp.einsum("stw,stv->wv", panel, chosen, precision=lax.Precision.HIGHEST)
        diag_pieces.append(diag_inverse[supernode] + extra)
    return jnp.stack(off_pieces), jnp.stack(diag_pieces)
```

```python
import functools

import jax
import jax.numpy as jnp
from jax import lax
from jax.experimental import pallas as pl
from jax.experimental.pallas import tpu as pltpu
from jax.sharding import PartitionSpec as P


AXES = ("row", "col")
TILE = 256
DEPTH = 4

SWAPPED = (0, 2, 1, 3)


def relative(place, odd):
    return jnp.where(odd, SWAPPED[place], place)


class Wires:
    def __init__(self, rows, cols):
        self.rows, self.cols = rows, cols

    def pairs(self, row_mask, col_mask=0):
        pick = row_mask if callable(row_mask) else lambda c: row_mask
        return [
            (r * self.cols + c, (r ^ pick(c)) * self.cols + (c ^ col_mask))
            for r in range(self.rows)
            for c in range(self.cols)
        ]

    def first(self, x):
        return lax.ppermute(x, AXES, self.pairs(lambda c: 1 + c % 2))

    def second(self, x):
        return lax.ppermute(x, AXES, self.pairs(lambda c: 2 - c % 2))

    def square(self, x, mask):
        return lax.ppermute(x, AXES, self.pairs(mask))

    def sibling(self, x, mask):
        return lax.ppermute(x, AXES, self.pairs(0, mask))


def split(x):
    high = x.astype(jnp.bfloat16)
    low = (x - high.astype(jnp.float32)).astype(jnp.bfloat16)
    return high, low


def triple(left, right):
    dot = functools.partial(jnp.dot, preferred_element_type=jnp.float32)
    return dot(left[0], right[0]) + (dot(left[0], right[1]) + dot(left[1], right[0]))


def product_kernel(
    plan, spot_ref, list_ref, ancestor, panels, *refs
):
    (places, n_pieces, supers, slots, rows, cols, row_tiles, col_tiles, unit, part, chunk) = plan
    pieces = refs[:n_pieces]
    product_out, own_out = refs[n_pieces : n_pieces + 2]
    (panel, total, blocks, square, pack, active, work, sem_p, sem_a, sem_o) = refs[-10:]
    r, c = spot_ref[0], spot_ref[1]
    odd = (c % 2) == 1

    def clear(n, _):
        active[n] = -1
        return 0

    lax.fori_loop(0, supers * row_tiles, clear, 0)

    def mark(n, _):
        t = list_ref[n // slots, n % slots]
        near = t - r * row_tiles

        @pl.when((t >= 0) & (near >= 0) & (near < row_tiles))
        def _():
            active[(n // slots) * row_tiles + near] = n % slots

        return 0

    lax.fori_loop(0, supers * slots, mark, 0)

    def busy(k):
        any_row = active[k * row_tiles] >= 0
        for i in range(1, row_tiles):
            any_row = any_row | (active[k * row_tiles + i] >= 0)
        return any_row

    def append(n, count):
        k, s = n // slots, n % slots
        t = list_ref[k, s]
        mine = (t >= 0) & (t // col_tiles == c)
        for i in range(row_tiles):
            take = mine & (active[k * row_tiles + i] >= 0)

            @pl.when(take)
            def _():
                work[count] = (k * slots + s) * row_tiles + i

            count = count + take.astype(jnp.int32)
        return count

    count = lax.fori_loop(0, supers * slots, append, jnp.int32(0))

    def fetch(w):
        item = work[w]
        i = item % row_tiles
        k, s = item // row_tiles // slots, (item // row_tiles) % slots
        col = pl.multiple_of((list_ref[k, s] - c * col_tiles) * TILE, TILE)
        row = pl.multiple_of(i * TILE, TILE)
        slot = w % DEPTH
        return pltpu.make_async_copy(
            ancestor.at[pl.ds(row, TILE), pl.ds(col, TILE)], blocks.at[slot], sem_a.at[slot]
        )

    for w in range(DEPTH):

        @pl.when(w < count)
        def _():
            fetch(w).start()

    def panel_copies(place, k, go):
        parts, mask, spot = place
        source = r ^ mask ^ relative(spot, odd)
        s = source * unit // TILE
        t = list_ref[k, s]
        wanted = (t >= 0) & busy(k) & ((t // col_tiles == c) | (t // row_tiles == r))

        @pl.when(wanted)
        def _():
            for kind, (piece, index, offset, size, col_mask) in enumerate(parts):
                start = source * unit
                if col_mask is not None:
                    start = start + (c ^ col_mask) * part
                start = pl.multiple_of(start + offset, 8)
                ref = panels if piece is None else pieces[piece]
                src = ref.at[k] if index is None else ref.at[index, k]
                copy = pltpu.make_async_copy(
                    src, panel.at[k, pl.ds(start, size), :], sem_p.at[kind, k * rows + source]
                )
                if go:
                    copy.start()
                else:
                    copy.wait()

    for go in (True, False):
        for place in places:

            def each(k, _, place=place, go=go):
                panel_copies(place, k, go)
                return 0

            lax.fori_loop(0, supers, each, 0)
        if go:
            total[...] = jnp.zeros_like(total)

    def multiply(w, _):
        item = work[w]
        i = item % row_tiles
        k, s = item // row_tiles // slots, (item // row_tiles) % slots
        slot = w % DEPTH
        fetch(w).wait()
        left = split(blocks[slot])
        right = split(panel[k, pl.ds(pl.multiple_of(s * TILE, TILE), TILE), :])
        here = pl.ds(pl.multiple_of(i * TILE, TILE), TILE)
        total[k, here, :] = total[k, here, :] + triple(left, right)

        @pl.when(w + DEPTH < count)
        def _():
            fetch(w + DEPTH).start()

        return 0

    lax.fori_loop(0, count, multiply, 0)

    keep = total.shape[1] // cols
    grain = min(TILE, keep)

    def results(k, go):
        for b in range(total.shape[1] // grain):
            owner = b * grain // keep
            copy = pltpu.make_async_copy(
                total.at[k, pl.ds(b * grain, grain), :],
                product_out.at[owner ^ c, k, pl.ds(b * grain % keep, grain), :],
                sem_o.at[b],
            )
            if go:
                copy.start()
            else:
                copy.wait()

    half = TILE // 2

    def corner(k, _):
        square[...] = jnp.zeros_like(square)
        for i in range(row_tiles):
            s = active[k * row_tiles + i]

            @pl.when(s >= 0)
            def _():
                near = panel[k, pl.ds(pl.multiple_of(s * TILE, TILE), TILE), :]
                square[...] += triple(split(near.T), split(total[k, pl.ds(i * TILE, TILE), :]))

        base = pl.multiple_of(k * 3 * half, half)
        pack[pl.ds(base, half), :] = square[:half, :half]
        pack[pl.ds(base + half, half), :] = square[:half, half:]
        pack[pl.ds(base + 2 * half, half), :] = square[half:, half:]
        return 0

    def emit(k, _):
        results(k, True)
        results(k, False)
        return 0

    lax.fori_loop(0, supers, corner, 0)

    def corner_copies(go):
        for mask in range(cols):
            for place in range(4):
                owner = c ^ mask
                spot = (r & 3) ^ relative(place, (owner % 2) == 1)
                copy = pltpu.make_async_copy(
                    pack.at[pl.ds(pl.multiple_of((owner * 4 + spot) * chunk, 8), chunk), :],
                    own_out.at[mask, SWAPPED[place]],
                    sem_o.at[mask * 4 + place],
                )
                if go:
                    copy.start()
                else:
                    copy.wait()

    corner_copies(True)
    corner_copies(False)
    lax.fori_loop(0, supers, emit, 0)


def corner_kernel(cols, chunk, spot_ref, inverse, *refs):
    parts, out, pack = refs[:cols], refs[cols], refs[cols + 1]
    r, c = spot_ref[0], spot_ref[1]
    for mask in range(cols):
        owner = c ^ mask
        for place in range(4):
            spot = (r & 3) ^ relative(place, (owner % 2) == 1)
            start = pl.multiple_of((owner * 4 + spot) * chunk, 8)
            pack[pl.ds(start, chunk), :] = parts[mask][place]
    half = inverse.shape[1] // 2
    for k in range(inverse.shape[0]):
        base = k * 3 * half
        cross = pack[base + half : base + 2 * half, :]
        out[k, :half, :half] = inverse[k, :half, :half] + pack[base : base + half, :]
        out[k, :half, half:] = inverse[k, :half, half:] + cross
        out[k, half:, :half] = inverse[k, half:, :half] + cross.T
        out[k, half:, half:] = inverse[k, half:, half:] + pack[base + 2 * half : base + 3 * half, :]


def local(ancestor, panels, tile_lists, diag_inverse):
    rows, cols = lax.axis_size("row"), lax.axis_size("col")
    r, c = lax.axis_index("row"), lax.axis_index("col")
    spot = jnp.stack([r, c]).astype(jnp.int32)
    wires = Wires(rows, cols)
    supers, unit, width = panels.shape
    slots = tile_lists.shape[1]
    part = unit // cols
    share = part // 8 // 8 * 8
    early = part - share
    masks = [4 * m for m in range(1, rows // 4)]

    mine = lax.dynamic_slice_in_dim(panels, c * part, part, 1)
    front = mine[:, :early]
    far = {}
    near1, pair, near2 = {}, {}, {}
    near1[0] = wires.first(mine)
    for m in masks:
        far[m] = wires.square(front, m)
    pair[0] = jnp.stack([mine, near1[0]])
    near2[0] = wires.second(pair[0])
    tails = {}
    for n, m in enumerate(masks):
        near1[m] = wires.first(far[m])
        if n == 0 and share:
            whole = jnp.concatenate([pair[0][:, :, early:], near2[0][:, :, early:]])
            for q in masks:
                tails[q] = wires.square(whole, q)
        pair[m] = jnp.stack([far[m], near1[m]])
        near2[m] = wires.second(pair[m])

    pieces = []

    def add(x):
        pieces.append(x)
        return len(pieces) - 1

    places = [[[], m, p] for m in [0] + masks for p in range(4)]
    where = {(m, p): parts for parts, m, p in places}
    where[0, 0].append((None, None, 0, unit, None))
    for m in [0] + masks:
        length = part if m == 0 else early
        groups = [(pair[m], (0, 1), 0, length), (near2[m], (2, 3), 0, length)]
        if m and share:
            groups.append((tails[m], (0, 1, 2, 3), early, share))
        for array, spots, offset, size in groups:
            for col_mask in range(cols):
                piece = add(array if col_mask == 0 else wires.sibling(array, col_mask))
                for index, p in enumerate(spots):
                    held = p if col_mask % 2 == 0 else SWAPPED[p]
                    if (m, held) != (0, 0):
                        where[m, held].append((piece, index, offset, size, col_mask))
    kinds = max(len(parts) for parts, _, _ in places)

    row_tiles, col_tiles = ancestor.shape[0] // TILE, ancestor.shape[1] // TILE
    keep = ancestor.shape[0] // cols
    packed = supers * 3 * (width // 2)
    chunk = packed // (4 * cols)
    plan = (places, len(pieces), supers, slots, rows, cols, row_tiles, col_tiles, unit, part, chunk)
    smem = pl.BlockSpec(memory_space=pltpu.SMEM)
    anywhere = pl.BlockSpec(memory_space=pl.ANY)
    product, corner = pl.pallas_call(
        functools.partial(product_kernel, plan),
        out_shape=(
            jax.ShapeDtypeStruct((cols, supers, keep, width), jnp.float32),
            jax.ShapeDtypeStruct((cols, 4, chunk, width // 2), jnp.float32),
        ),
        in_specs=[smem, smem] + [anywhere] * (2 + len(pieces)),
        out_specs=(anywhere, anywhere),
        scratch_shapes=[
            pltpu.VMEM((supers, slots * TILE, width), jnp.float32),
            pltpu.VMEM((supers, row_tiles * TILE, width), jnp.float32),
            pltpu.VMEM((DEPTH, TILE, TILE), jnp.float32),
            pltpu.VMEM((width, width), jnp.float32),
            pltpu.VMEM((packed, width // 2), jnp.float32),
            pltpu.SMEM((supers * row_tiles,), jnp.int32),
            pltpu.SMEM((supers * slots * row_tiles,), jnp.int32),
            pltpu.SemaphoreType.DMA((kinds, supers * rows)),
            pltpu.SemaphoreType.DMA((DEPTH,)),
            pltpu.SemaphoreType.DMA((max(4 * cols, row_tiles * TILE // min(TILE, keep)),)),
        ],
        compiler_params=pltpu.CompilerParams(vmem_limit_bytes=48 * 2**20),
        name="listed_product",
    )(spot, tile_lists, ancestor, panels, *pieces)

    sums = corner[0]
    for mask in range(1, cols):
        sums = sums + wires.sibling(corner[mask], mask)
    sums = sums[:2] + wires.first(sums[2:])
    sums = sums[0] + wires.second(sums[1])
    for m in masks:
        if m & (m - 1) == 0:
            sums = sums + wires.square(sums, m)
    both = jnp.stack([sums, wires.second(sums)])
    others = wires.first(both)
    full = jnp.stack([both[0], others[0], both[1], others[1]])
    parts = [full] + [wires.sibling(full, mask) for mask in range(1, cols)]
    block = product[0]
    for mask in range(1, cols):
        block = block + wires.sibling(product[mask], mask)
    vmem = pl.BlockSpec(memory_space=pltpu.VMEM)
    diag = pl.pallas_call(
        functools.partial(corner_kernel, cols, chunk),
        out_shape=jax.ShapeDtypeStruct(diag_inverse.shape, jnp.float32),
        in_specs=[smem] + [vmem] * (1 + cols),
        out_specs=vmem,
        scratch_shapes=[pltpu.VMEM((packed, width // 2), jnp.float32)],
        name="corner_blocks",
    )(spot, diag_inverse, *parts)
    return -block, diag


def solution(mesh):
    in_specs = (P("row", "col"), P(None, "row", None), P(), P())
    out_specs = (P(None, ("row", "col"), None), P())
    return jax.shard_map(local, mesh=mesh, in_specs=in_specs, out_specs=out_specs, check_vma=False)
```

```python
import functools

import jax
import jax.numpy as jnp
from jax import lax
from jax.experimental import pallas as pl
from jax.experimental.pallas import tpu as pltpu
from jax.sharding import PartitionSpec as P


AXES = ("row", "col")
TILE = 256
DEPTH = 12
TOGETHER = 4
SHARE = 24

SWAPPED = (0, 2, 1, 3)


def relative(place, odd):
    return jnp.where(odd, SWAPPED[place], place)


class Wires:
    def __init__(self, rows, cols):
        self.rows, self.cols = rows, cols

    def pairs(self, row_mask, col_mask=0, squares=None):
        pick = row_mask if callable(row_mask) else lambda c: row_mask
        return [
            (r * self.cols + c, (r ^ pick(c)) * self.cols + (c ^ col_mask))
            for r in range(self.rows)
            for c in range(self.cols)
            if squares is None or r // 4 in squares
        ]

    def first(self, x):
        return lax.ppermute(x, AXES, self.pairs(lambda c: 1 + c % 2))

    def second(self, x):
        return lax.ppermute(x, AXES, self.pairs(lambda c: 2 - c % 2))

    def square(self, x, mask, squares=None):
        return lax.ppermute(x, AXES, self.pairs(mask, squares=squares))

    def sibling(self, x, mask):
        return lax.ppermute(x, AXES, self.pairs(0, mask))


def over(x, d):
    return x >> (d.bit_length() - 1) if d & (d - 1) == 0 else x // d


def rest(x, d):
    return x & (d - 1) if d & (d - 1) == 0 else x % d


def split(x):
    high = x.astype(jnp.bfloat16)
    low = (x - high.astype(jnp.float32)).astype(jnp.bfloat16)
    return high, low


def left_of(x):
    high, low = split(x)
    return jnp.concatenate([low, high, high], axis=1)


def right_of(x):
    high, low = split(x)
    return jnp.concatenate([high, low, high], axis=0)


def dot(left, right):
    return jnp.dot(left, right, preferred_element_type=jnp.float32)


class Plan:
    def __init__(self, supers, rows, row_tiles):
        self.most = supers * rows
        self.counts = 0
        self.head = 2
        self.rows = self.head + supers + 1
        self.slots = self.rows + supers * row_tiles
        self.wanted = self.slots + supers * row_tiles
        self.only = self.wanted + self.most
        self.works = self.only + self.most
        self.size = self.works + self.most * row_tiles + TOGETHER


def square_base(r, masks):
    square = over(r, 4)
    inner = (square == 1) | (square == 2)
    return (r ^ jnp.where(inner, masks[0], masks[1])) & ~3, inner


def plan_kernel(plan, rows, unit, row_tiles, col_tiles, spot_ref, list_ref, out):
    r, c = spot_ref[0], spot_ref[1]
    supers, slots = list_ref.shape

    def rows_of(n, count):
        k, s = over(n, slots), rest(n, slots)
        t = list_ref[k, s]
        take = over(t, row_tiles) == r

        @pl.when(s == 0)
        def _():
            out[plan.head + k] = count

        @pl.when(take)
        def _():
            out[plan.rows + count] = k * row_tiles + rest(t, row_tiles)
            out[plan.slots + count] = s

        return count + take.astype(jnp.int32)

    out[plan.head + supers] = lax.fori_loop(0, supers * slots, rows_of, jnp.int32(0))

    def scan(n, counts):
        works, only = counts
        k, source = over(n, rows), rest(n, rows)
        t = list_ref[k, over(source * unit, TILE)]
        low, high = out[plan.head + k], out[plan.head + k + 1]
        near = over(t, row_tiles) == r
        here = (over(t, col_tiles) == c) & (high > low)
        lone = near & jnp.logical_not(here)
        out[plan.wanted + n] = (near | here).astype(jnp.int32)

        @pl.when(lone)
        def _():
            out[plan.only + only] = n

        def append(j, works):
            out[plan.works + works] = n * row_tiles + rest(out[plan.rows + j], row_tiles)
            return works + 1

        works = lax.fori_loop(low, jnp.where(here, high, low), append, works)
        return works, only + lone.astype(jnp.int32)

    works, only = lax.fori_loop(0, supers * rows, scan, (jnp.int32(0), jnp.int32(0)))
    for extra in range(TOGETHER - 1):
        out[plan.works + works + extra] = out[plan.works + jnp.maximum(works - 1, 0)]
    out[plan.counts] = works
    out[plan.counts + 1] = only


def product_kernel(statics, spot_ref, list_ref, plan_ref, ancestor, panels, *refs):
    (plan, parts, n_pieces, rows, cols, col_tiles, part, chunk) = statics
    supers, unit, width = panels.shape
    row_tiles = ancestor.shape[0] // TILE
    keep = ancestor.shape[0] // cols
    half = width // 2
    pieces, outs = refs[:n_pieces], refs[n_pieces : n_pieces + 3 * cols]
    (panel, total, blocks, zeros, corner, pack, sem_p, sem_a, sem_o, sem_c) = refs[
        n_pieces + 3 * cols :
    ]
    r, c = spot_ref[0], spot_ref[1]
    odd = (c % 2) == 1
    n_rows, n_works = plan_ref[plan.head + supers], plan_ref[plan.counts]

    def loop(count, body):
        def step(n, _):
            body(n)
            return 0

        lax.fori_loop(0, count, step, 0)

    def tile_rows(i):
        return pl.ds(pl.multiple_of(i * TILE, TILE), TILE)

    def work_of(w):
        code = plan_ref[plan.works + w]
        return over(code, row_tiles), rest(code, row_tiles)

    def fetch(w):
        n, i = work_of(w)
        k, source = over(n, rows), rest(n, rows)
        t = list_ref[k, over(source * unit, TILE)]
        col = pl.multiple_of((t - c * col_tiles) * TILE + rest(source * unit, TILE), min(unit, TILE))
        slot = lax.rem(w, DEPTH)
        return pltpu.make_async_copy(
            ancestor.at[tile_rows(i), pl.ds(col, unit)], blocks.at[slot], sem_a.at[slot]
        )

    for masks, place, entries in parts:
        base, inner = square_base(r, masks)
        source = base + ((r & 3) ^ relative(place, odd))

        def start_panels(k, entries=entries, inner=inner, source=source):
            n = k * rows + source

            @pl.when(plan_ref[plan.wanted + n] != 0)
            def _():
                for piece, index, offset, size, side, where_inner in entries:

                    def go(piece=piece, index=index, offset=offset, size=size, side=side):
                        start = source * unit + offset
                        if side is not None:
                            start = start + (c ^ side) * part
                        ref = panels if piece is None else pieces[piece]
                        pltpu.make_async_copy(
                            ref.at[k] if index is None else ref.at[index, k],
                            panel.at[k, pl.ds(pl.multiple_of(start, 8), size), :],
                            sem_p.at[n],
                        ).start()

                    if where_inner is None:
                        go()
                    else:
                        pl.when(inner == where_inner)(go)

        loop(supers, start_panels)

    for w in range(DEPTH):
        pl.when(w < n_works)(lambda w=w: fetch(w).start())

    def unit_of(n):
        return panel.at[over(n, rows), pl.ds(pl.multiple_of(rest(n, rows) * unit, unit), unit), :]

    def wait_panel(n):
        pltpu.make_async_copy(panels.at[0], unit_of(n), sem_p.at[n]).wait()

    zeros[...] = jnp.zeros_like(zeros)

    def clear(n):
        code = plan_ref[plan.rows + n]
        k, i = over(code, row_tiles), rest(code, row_tiles)
        total[k, tile_rows(i), :] = jnp.zeros((TILE, width), jnp.float32)

    loop(n_rows, clear)

    grain = min(TILE, keep)
    grains = TILE // grain

    def result(k, row, ref, sem, go):
        target_rows = pl.ds(pl.multiple_of(rest(row, keep), grain), grain)
        for mask in range(cols):

            @pl.when(over(row, keep) ^ c == mask)
            def _():
                copy = pltpu.make_async_copy(ref, outs[mask].at[k, target_rows, :], sem)
                copy.start() if go else copy.wait()

    def listed(n, go):
        code = plan_ref[plan.rows + n]
        k, i = over(code, row_tiles), rest(code, row_tiles)
        for g in range(grains):
            row = i * TILE + g * grain
            ref = total.at[k, pl.ds(pl.multiple_of(row, grain), grain), :]
            result(k, row, ref, sem_o.at[code * grains + g], go)

    def blank(code, go):
        k, i = over(code, row_tiles), rest(code, row_tiles)
        low, high = plan_ref[plan.head + k], plan_ref[plan.head + k + 1]
        hit = lax.fori_loop(
            low, high, lambda n, h: h | (plan_ref[plan.rows + n] == code).astype(jnp.int32), jnp.int32(0)
        )

        @pl.when(hit == 0)
        def _():
            for g in range(grains):
                result(k, i * TILE + g * grain, zeros, sem_o.at[code * grains + g], go)

    loop(supers * row_tiles, lambda n: blank(n, True))

    def multiply(v, before):
        first = v * TOGETHER
        sums, spots = [], []
        for w in range(TOGETHER):
            n, _ = work_of(first + w)
            pl.when(before != n)(lambda n=n: wait_panel(n))
            pl.when(first + w < n_works)(lambda w=w: fetch(first + w).wait())
            before = n
        for w in range(TOGETHER):
            n, i = work_of(first + w)
            block = blocks[lax.rem(first + w, DEPTH)]
            if w:
                block = jnp.where(first + w < n_works, block, 0.0)
            sums.append(dot(left_of(block), right_of(unit_of(n)[...])))
            spots.append((over(n, rows), i))
        for (k, i), x in zip(spots, sums):
            total[k, tile_rows(i), :] += x
        for w in range(TOGETHER):
            later = first + w + DEPTH
            pl.when(later < n_works)(lambda later=later: fetch(later).start())
        return before

    lax.fori_loop(0, (n_works + TOGETHER - 1) // TOGETHER, multiply, jnp.int32(-1))
    loop(n_rows, lambda n: listed(n, True))
    loop(plan_ref[plan.counts + 1], lambda m: wait_panel(plan_ref[plan.only + m]))

    def corners(k, _):
        corner[...] = jnp.zeros_like(corner)

        def one(n, _):
            here = tile_rows(rest(plan_ref[plan.rows + n], row_tiles))
            near = panel[k, tile_rows(plan_ref[plan.slots + n]), :]
            corner[...] += dot(left_of(near.T), right_of(total[k, here, :]))
            return 0

        lax.fori_loop(plan_ref[plan.head + k], plan_ref[plan.head + k + 1], one, 0)
        start = pl.multiple_of(k * 3 * half, half)
        pack[pl.ds(start, half), :] = corner[:half, :half]
        pack[pl.ds(start + half, half), :] = corner[:half, half:]
        pack[pl.ds(start + 2 * half, half), :] = corner[half:, half:]
        return 0

    lax.fori_loop(0, supers, corners, 0)

    def corner_copies(go):
        for mask in range(cols):
            for place in range(4):
                owner = c ^ mask
                spot = (r & 3) ^ relative(place, (owner % 2) == 1)
                copy = pltpu.make_async_copy(
                    pack.at[pl.ds(pl.multiple_of((owner * 4 + spot) * chunk, 8), chunk), :],
                    outs[cols + 2 * mask + place % 2].at[place // 2],
                    sem_c.at[mask * 4 + place],
                )
                copy.start() if go else copy.wait()

    corner_copies(True)
    corner_copies(False)
    loop(n_rows, lambda n: listed(n, False))
    loop(supers * row_tiles, lambda n: blank(n, False))


def corner_kernel(cols, chunk, spot_ref, inverse, *refs):
    parts, out, pack = refs[:cols], refs[cols], refs[cols + 1]
    r, c = spot_ref[0], spot_ref[1]
    for mask in range(cols):
        owner = c ^ mask
        for place in range(4):
            spot = (r & 3) ^ relative(place, (owner % 2) == 1)
            start = pl.multiple_of((owner * 4 + spot) * chunk, 8)
            pack[pl.ds(start, chunk), :] = parts[mask][place]
    half = inverse.shape[1] // 2
    for k in range(inverse.shape[0]):
        base = k * 3 * half
        cross = pack[base + half : base + 2 * half, :]
        out[k, :half, :half] = inverse[k, :half, :half] + pack[base : base + half, :]
        out[k, :half, half:] = inverse[k, :half, half:] + cross
        out[k, half:, :half] = inverse[k, half:, :half] + cross.T
        out[k, half:, half:] = inverse[k, half:, half:] + pack[base + 2 * half : base + 3 * half, :]


def local(ancestor, panels, tile_lists, diag_inverse):
    rows, cols = lax.axis_size("row"), lax.axis_size("col")
    r, c = lax.axis_index("row"), lax.axis_index("col")
    spot = jnp.stack([r, c]).astype(jnp.int32)
    wires = Wires(rows, cols)
    supers, unit, width = panels.shape
    slots = tile_lists.shape[1]
    row_tiles, col_tiles = ancestor.shape[0] // TILE, ancestor.shape[1] // TILE
    part = unit // cols
    share = part * SHARE // 128 // 8 * 8
    early = part - share
    masks = [4 * m for m in range(1, rows // 4)]

    mine = lax.dynamic_slice_in_dim(panels, c * part, part, 1)
    front = lax.dynamic_slice_in_dim(panels, c * part, early, 1)

    def around(held):
        near = wires.first(held)
        return [held, near, wires.second(held), wires.second(near)]

    own = around(mine)

    if rows == 16:
        inner = (r // 4 == 1) | (r // 4 == 2)
        z1 = wires.square(front, 4)
        z2 = wires.square(front, 12, (1, 2))
        z3 = wires.square(z1, 12, (1, 2))
        z4 = wires.square(z2, 4, (1, 2))
        z5 = wires.square(z3, 4, (1, 2))
        far = [((4, 4), z1), ((12, 8), jnp.where(inner, z2, z4)), ((8, 12), jnp.where(inner, z3, z5))]
    else:
        far = [((m, m), wires.square(front, m)) for m in masks]
    ends = jnp.stack([x[:, early:] for x in own])
    tails = {m: wires.square(ends, m) for m in masks}
    sides = range(1, cols)
    tails = {m: [x] + [wires.sibling(x, s) for s in sides] for m, x in tails.items()}

    smem = pl.BlockSpec(memory_space=pltpu.SMEM)
    anywhere = pl.BlockSpec(memory_space=pltpu.HBM)
    keep = ancestor.shape[0] // cols
    packed = supers * 3 * (width // 2)
    chunk = packed // (4 * cols)
    grains = row_tiles * (TILE // min(TILE, keep))
    finals = [jax.ShapeDtypeStruct((supers, keep, width), jnp.float32)] * cols
    finals += [jax.ShapeDtypeStruct((2, chunk, width // 2), jnp.float32)] * (2 * cols)
    items = [((0, 0), own)] + [(m, around(held)) for m, held in far]
    plan = Plan(supers, rows, row_tiles)
    planner = pl.pallas_call(
        functools.partial(plan_kernel, plan, rows, unit, row_tiles, col_tiles),
        out_shape=jax.ShapeDtypeStruct((plan.size,), jnp.int32),
        in_specs=[smem, smem],
        out_specs=smem,
        name="plan",
    )
    lists = planner(spot, tile_lists)
    arrays, parts = [], []
    for n, (square_masks, groups) in enumerate(items):
        entries = [[] for _ in range(4)]
        for p, array in enumerate(groups):
            if n == 0 and p == 0:
                entries[0].append((None, None, 0, unit, None, None))
                continue
            copies = [array] + [wires.sibling(array, s) for s in sides]
            for s, copy in enumerate(copies):
                entry = (len(arrays), None, 0, array.shape[1], s, None)
                entries[SWAPPED[p] if s % 2 else p].append(entry)
                arrays.append(copy)
        if n and share:
            choices = [(square_masks[0], None)]
            if square_masks[0] != square_masks[1]:
                choices = [(square_masks[0], True), (square_masks[1], False)]
            for m, flag in choices:
                for s, copy in enumerate(tails[m]):
                    if all(copy is not x for x in arrays):
                        arrays.append(copy)
                    at = [copy is x for x in arrays].index(True)
                    for p in range(4):
                        entries[SWAPPED[p] if s % 2 else p].append((at, p, early, share, s, flag))
        parts += [(square_masks, p, entries[p]) for p in range(4)]
    statics = (plan, parts, len(arrays), rows, cols, col_tiles, part, chunk)
    scratch = [
        pltpu.VMEM((supers, slots * TILE, width), jnp.float32),
        pltpu.VMEM((supers, row_tiles * TILE, width), jnp.float32),
        pltpu.VMEM((DEPTH, TILE, unit), jnp.float32),
        pltpu.VMEM((min(TILE, keep), width), jnp.float32),
        pltpu.VMEM((width, width), jnp.float32),
        pltpu.VMEM((packed, width // 2), jnp.float32),
        pltpu.SemaphoreType.DMA((supers * rows,)),
        pltpu.SemaphoreType.DMA((DEPTH,)),
        pltpu.SemaphoreType.DMA((supers * grains,)),
        pltpu.SemaphoreType.DMA((4 * cols,)),
    ]
    call = pl.pallas_call(
        functools.partial(product_kernel, statics),
        out_shape=tuple(finals),
        in_specs=[smem] * 3 + [anywhere] * (2 + len(arrays)),
        out_specs=(anywhere,) * len(finals),
        scratch_shapes=scratch,
        compiler_params=pltpu.CompilerParams(vmem_limit_bytes=67043328),
        name="listed_products",
    )
    carried = call(spot, tile_lists, lists, ancestor, panels, *arrays)
    product, corner = carried[:cols], carried[cols:]

    low, high = corner[0], corner[1]
    for m in sides:
        high = high + wires.sibling(corner[2 * m + 1], m)
    high = wires.first(high)
    for m in sides:
        low = low + wires.sibling(corner[2 * m], m)
    sums = low + high
    sums = sums[0] + wires.second(sums[1])
    for m in masks:
        if m & (m - 1) == 0:
            sums = sums + wires.square(sums, m)
    both = jnp.stack([sums, wires.second(sums)])
    others = wires.first(both)
    full = jnp.stack([both[0], others[0], both[1], others[1]])
    parts = [full] + [wires.sibling(full, s) for s in sides]
    moved = [wires.sibling(product[s], s) for s in sides]
    block = product[0]
    for x in moved:
        block = block + x
    block = -block
    vmem = pl.BlockSpec(memory_space=pltpu.VMEM)
    diag = pl.pallas_call(
        functools.partial(corner_kernel, cols, chunk),
        out_shape=jax.ShapeDtypeStruct(diag_inverse.shape, jnp.float32),
        in_specs=[smem] + [vmem] * (1 + cols),
        out_specs=vmem,
        scratch_shapes=[pltpu.VMEM((packed, width // 2), jnp.float32)],
        name="corner_blocks",
    )(spot, diag_inverse, *parts)
    return block, diag


def solution(mesh):
    in_specs = (P("row", "col"), P(None, "row", None), P(), P())
    out_specs = (P(None, ("row", "col"), None), P())
    return jax.shard_map(local, mesh=mesh, in_specs=in_specs, out_specs=out_specs, check_vma=False)
```

```python
import functools

import jax
import jax.numpy as jnp
from jax import lax
from jax.experimental import pallas as pl
from jax.experimental.pallas import tpu as pltpu
from jax.sharding import PartitionSpec as P


AXES = ("row", "col")
TILE = 256
DEPTH = 12
TOGETHER = 4
SHARE = 24

SWAPPED = (0, 2, 1, 3)


def relative(place, odd):
    return jnp.where(odd, SWAPPED[place], place)


class Wires:
    def __init__(self, rows, cols):
        self.rows, self.cols = rows, cols

    def pairs(self, row_mask, col_mask=0, squares=None):
        pick = row_mask if callable(row_mask) else lambda c: row_mask
        return [
            (r * self.cols + c, (r ^ pick(c)) * self.cols + (c ^ col_mask))
            for r in range(self.rows)
            for c in range(self.cols)
            if squares is None or r // 4 in squares
        ]

    def first(self, x):
        return lax.ppermute(x, AXES, self.pairs(lambda c: 1 + c % 2))

    def second(self, x):
        return lax.ppermute(x, AXES, self.pairs(lambda c: 2 - c % 2))

    def square(self, x, mask, squares=None):
        return lax.ppermute(x, AXES, self.pairs(mask, squares=squares))

    def sibling(self, x, mask):
        return lax.ppermute(x, AXES, self.pairs(0, mask))


def over(x, d):
    return x >> (d.bit_length() - 1) if d & (d - 1) == 0 else x // d


def rest(x, d):
    return x & (d - 1) if d & (d - 1) == 0 else x % d


def split(x):
    high = x.astype(jnp.bfloat16)
    low = (x - high.astype(jnp.float32)).astype(jnp.bfloat16)
    return high, low


def left_of(x):
    high, low = split(x)
    return jnp.concatenate([low, high, high], axis=1)


def right_of(x):
    high, low = split(x)
    return jnp.concatenate([high, low, high], axis=0)


def dot(left, right):
    return jnp.dot(left, right, preferred_element_type=jnp.float32)


class Plan:
    def __init__(self, supers, rows, row_tiles):
        self.most = supers * rows
        self.counts = 0
        self.head = 2
        self.rows = self.head + supers + 1
        self.slots = self.rows + supers * row_tiles
        self.wanted = self.slots + supers * row_tiles
        self.only = self.wanted + self.most
        self.works = self.only + self.most
        self.size = self.works + self.most * row_tiles + TOGETHER


def square_base(r, masks):
    square = over(r, 4)
    inner = (square == 1) | (square == 2)
    return (r ^ jnp.where(inner, masks[0], masks[1])) & ~3, inner


def plan_kernel(plan, squares, rows, unit, row_tiles, col_tiles, spot_ref, list_ref, out):
    r, c = spot_ref[0], spot_ref[1]
    supers, slots = list_ref.shape

    def rows_of(n, count):
        k, s = over(n, slots), rest(n, slots)
        t = list_ref[k, s]
        take = over(t, row_tiles) == r

        @pl.when(s == 0)
        def _():
            out[plan.head + k] = count

        @pl.when(take)
        def _():
            out[plan.rows + count] = k * row_tiles + rest(t, row_tiles)
            out[plan.slots + count] = s

        return count + take.astype(jnp.int32)

    out[plan.head + supers] = lax.fori_loop(0, supers * slots, rows_of, jnp.int32(0))

    odd = (c % 2) == 1
    works, only = jnp.int32(0), jnp.int32(0)
    for masks in squares:
        base, _ = square_base(r, masks)
        for place in range(4):
            source = base + ((r & 3) ^ relative(place, odd))

            def each(k, counts, source=source):
                works, only = counts
                n = k * rows + source
                t = list_ref[k, over(source * unit, TILE)]
                low, high = out[plan.head + k], out[plan.head + k + 1]
                here = (over(t, col_tiles) == c) & (high > low)
                near = over(t, row_tiles) == r
                lone = near & jnp.logical_not(here)
                out[plan.wanted + n] = (here | near).astype(jnp.int32)

                @pl.when(lone)
                def _():
                    out[plan.only + only] = n

                def append(j, works):
                    out[plan.works + works] = n * row_tiles + rest(out[plan.rows + j], row_tiles)
                    return works + 1

                works = lax.fori_loop(low, jnp.where(here, high, low), append, works)
                return works, only + lone.astype(jnp.int32)

            works, only = lax.fori_loop(0, supers, each, (works, only))
    for extra in range(TOGETHER - 1):
        out[plan.works + works + extra] = out[plan.works + jnp.maximum(works - 1, 0)]
    out[plan.counts] = works
    out[plan.counts + 1] = only


def product_kernel(statics, spot_ref, list_ref, plan_ref, ancestor, panels, *refs):
    (plan, parts, n_pieces, rows, cols, col_tiles, part, chunk) = statics
    supers, unit, width = panels.shape
    row_tiles = ancestor.shape[0] // TILE
    keep = ancestor.shape[0] // cols
    half = width // 2
    pieces, outs = refs[:n_pieces], refs[n_pieces : n_pieces + 3 * cols]
    (panel, total, blocks, corner, pack, sem_p, sem_a, sem_o) = refs[
        n_pieces + 3 * cols :
    ]
    r, c = spot_ref[0], spot_ref[1]
    odd = (c % 2) == 1
    n_rows, n_works = plan_ref[plan.head + supers], plan_ref[plan.counts]

    def loop(count, body):
        def step(n, _):
            body(n)
            return 0

        lax.fori_loop(0, count, step, 0)

    def tile_rows(i):
        return pl.ds(pl.multiple_of(i * TILE, TILE), TILE)

    def work_of(w):
        code = plan_ref[plan.works + w]
        return over(code, row_tiles), rest(code, row_tiles)

    def fetch(w):
        n, i = work_of(w)
        k, source = over(n, rows), rest(n, rows)
        t = list_ref[k, over(source * unit, TILE)]
        col = pl.multiple_of((t - c * col_tiles) * TILE + rest(source * unit, TILE), min(unit, TILE))
        slot = lax.rem(w, DEPTH)
        return pltpu.make_async_copy(
            ancestor.at[tile_rows(i), pl.ds(col, unit)], blocks.at[slot], sem_a.at[slot]
        )

    for w in range(DEPTH):
        pl.when(w < n_works)(lambda w=w: fetch(w).start())

    for masks, place, entries in parts:
        base, inner = square_base(r, masks)
        source = base + ((r & 3) ^ relative(place, odd))


        def start_panels(k, entries=entries, inner=inner, source=source):
            n = k * rows + source

            @pl.when(plan_ref[plan.wanted + n] != 0)
            def _():
                for piece, index, offset, size, side, where_inner in entries:

                    def go(piece=piece, index=index, offset=offset, size=size, side=side):
                        start = source * unit + offset
                        if side is not None:
                            start = start + (c ^ side) * part
                        ref = panels if piece is None else pieces[piece]
                        pltpu.make_async_copy(
                            ref.at[k] if index is None else ref.at[index, k],
                            panel.at[k, pl.ds(pl.multiple_of(start, 8), size), :],
                            sem_p.at[n],
                        ).start()

                    if where_inner is None:
                        go()
                    else:
                        pl.when(inner == where_inner)(go)

        loop(supers, start_panels)

    def unit_of(n):
        return panel.at[over(n, rows), pl.ds(pl.multiple_of(rest(n, rows) * unit, unit), unit), :]

    def wait_panel(n):
        pltpu.make_async_copy(panels.at[0], unit_of(n), sem_p.at[n]).wait()

    def clear(n):
        code = plan_ref[plan.rows + n]
        k, i = over(code, row_tiles), rest(code, row_tiles)
        total[k, tile_rows(i), :] = jnp.zeros((TILE, width), jnp.float32)

    loop(n_rows, clear)

    grain = min(TILE, keep)
    grains = TILE // grain

    def result(k, row, ref, sem, go):
        target_rows = pl.ds(pl.multiple_of(rest(row, keep), grain), grain)
        for mask in range(cols):

            @pl.when(over(row, keep) ^ c == mask)
            def _():
                copy = pltpu.make_async_copy(ref, outs[mask].at[k, target_rows, :], sem)
                copy.start() if go else copy.wait()

    def listed(n, go):
        code = plan_ref[plan.rows + n]
        k, i = over(code, row_tiles), rest(code, row_tiles)
        for g in range(grains):
            row = i * TILE + g * grain
            ref = total.at[k, pl.ds(pl.multiple_of(row, grain), grain), :]
            result(k, row, ref, sem_o.at[code * grains + g], go)

    def multiply(v, before):
        first = v * TOGETHER
        sums, spots = [], []
        for w in range(TOGETHER):
            n, _ = work_of(first + w)
            pl.when(before != n)(lambda n=n: wait_panel(n))
            pl.when(first + w < n_works)(lambda w=w: fetch(first + w).wait())
            before = n
        for w in range(TOGETHER):
            n, i = work_of(first + w)
            block = blocks[lax.rem(first + w, DEPTH)]
            if w:
                block = jnp.where(first + w < n_works, block, 0.0)
            sums.append(dot(left_of(block), right_of(unit_of(n)[...])))
            spots.append((over(n, rows), i))
        for (k, i), x in zip(spots, sums):
            total[k, tile_rows(i), :] += x
        for w in range(TOGETHER):
            later = first + w + DEPTH
            pl.when(later < n_works)(lambda later=later: fetch(later).start())
        return before

    lax.fori_loop(0, (n_works + TOGETHER - 1) // TOGETHER, multiply, jnp.int32(-1))
    loop(n_rows, lambda n: listed(n, True))
    loop(plan_ref[plan.counts + 1], lambda m: wait_panel(plan_ref[plan.only + m]))

    def corners(k, _):
        corner[...] = jnp.zeros_like(corner)

        def product(n):
            here = tile_rows(rest(plan_ref[plan.rows + n], row_tiles))
            near = panel[k, tile_rows(plan_ref[plan.slots + n]), :]
            return dot(left_of(near.T), right_of(total[k, here, :]))

        low, high = plan_ref[plan.head + k], plan_ref[plan.head + k + 1]

        def two(n, _):
            corner[...] += product(low + 2 * n) + product(low + 2 * n + 1)
            return 0

        lax.fori_loop(0, (high - low) >> 1, two, 0)

        @pl.when(((high - low) & 1) == 1)
        def _():
            corner[...] += product(high - 1)

        start = pl.multiple_of(k * 3 * half, half)
        pack[pl.ds(start, half), :] = corner[:half, :half]
        pack[pl.ds(start + half, half), :] = corner[:half, half:]
        pack[pl.ds(start + 2 * half, half), :] = corner[half:, half:]
        return 0

    lax.fori_loop(0, supers, corners, 0)
    for mask in range(cols):
        for place in range(4):
            owner = c ^ mask
            spot = (r & 3) ^ relative(place, (owner % 2) == 1)
            rows_at = pl.ds(pl.multiple_of((owner * 4 + spot) * chunk, 8), chunk)
            outs[cols + 2 * mask + place % 2][place // 2] = pack[rows_at, :]
    loop(n_rows, lambda n: listed(n, False))


def corner_kernel(cols, chunk, spot_ref, inverse, *refs):
    parts, out, pack = refs[:cols], refs[cols], refs[cols + 1]
    r, c = spot_ref[0], spot_ref[1]
    for mask in range(cols):
        owner = c ^ mask
        for place in range(4):
            spot = (r & 3) ^ relative(place, (owner % 2) == 1)
            start = pl.multiple_of((owner * 4 + spot) * chunk, 8)
            pack[pl.ds(start, chunk), :] = parts[mask][place]
    half = inverse.shape[1] // 2
    for k in range(inverse.shape[0]):
        base = k * 3 * half
        cross = pack[base + half : base + 2 * half, :]
        out[k, :half, :half] = inverse[k, :half, :half] + pack[base : base + half, :]
        out[k, :half, half:] = inverse[k, :half, half:] + cross
        out[k, half:, :half] = inverse[k, half:, :half] + cross.T
        out[k, half:, half:] = inverse[k, half:, half:] + pack[base + 2 * half : base + 3 * half, :]


def local(ancestor, panels, tile_lists, diag_inverse):
    rows, cols = lax.axis_size("row"), lax.axis_size("col")
    r, c = lax.axis_index("row"), lax.axis_index("col")
    spot = jnp.stack([r, c]).astype(jnp.int32)
    wires = Wires(rows, cols)
    supers, unit, width = panels.shape
    slots = tile_lists.shape[1]
    row_tiles, col_tiles = ancestor.shape[0] // TILE, ancestor.shape[1] // TILE
    part = unit // cols
    share = part * SHARE // 128 // 8 * 8
    early = part - share
    masks = [4 * m for m in range(1, rows // 4)]

    mine = lax.dynamic_slice_in_dim(panels, c * part, part, 1)
    front = lax.dynamic_slice_in_dim(panels, c * part, early, 1)

    def around(held):
        near = wires.first(held)
        return [held, near, wires.second(held), wires.second(near)]

    own = around(mine)

    if rows == 16:
        inner = (r // 4 == 1) | (r // 4 == 2)
        z1 = wires.square(front, 4)
        z2 = wires.square(front, 12, (1, 2))
        z3 = wires.square(z1, 12, (1, 2))
        z4 = wires.square(z2, 4, (1, 2))
        z5 = wires.square(z3, 4, (1, 2))
        far = [((4, 4), z1), ((12, 8), jnp.where(inner, z2, z4)), ((8, 12), jnp.where(inner, z3, z5))]
    else:
        far = [((m, m), wires.square(front, m)) for m in masks]
    ends = jnp.stack([x[:, early:] for x in own])
    tails = {m: wires.square(ends, m) for m in masks}
    sides = range(1, cols)
    tails = {m: [x] + [wires.sibling(x, s) for s in sides] for m, x in tails.items()}

    smem = pl.BlockSpec(memory_space=pltpu.SMEM)
    anywhere = pl.BlockSpec(memory_space=pltpu.HBM)
    keep = ancestor.shape[0] // cols
    packed = supers * 3 * (width // 2)
    chunk = packed // (4 * cols)
    grains = row_tiles * (TILE // min(TILE, keep))
    finals = [jax.ShapeDtypeStruct((supers, keep, width), jnp.float32)] * cols
    finals += [jax.ShapeDtypeStruct((2, chunk, width // 2), jnp.float32)] * (2 * cols)
    items = [((0, 0), own)] + [(m, around(held)) for m, held in far]
    plan = Plan(supers, rows, row_tiles)
    planner = pl.pallas_call(
        functools.partial(plan_kernel, plan, [m for m, _ in items], rows, unit, row_tiles, col_tiles),
        out_shape=jax.ShapeDtypeStruct((plan.size,), jnp.int32),
        in_specs=[smem, smem],
        out_specs=smem,
        name="plan",
    )
    lists = planner(spot, tile_lists)
    arrays, parts = [], []
    for n, (square_masks, groups) in enumerate(items):
        entries = [[] for _ in range(4)]
        for p, array in enumerate(groups):
            if n == 0 and p == 0:
                entries[0].append((None, None, 0, unit, None, None))
                continue
            copies = [array] + [wires.sibling(array, s) for s in sides]
            for s, copy in enumerate(copies):
                entry = (len(arrays), None, 0, array.shape[1], s, None)
                entries[SWAPPED[p] if s % 2 else p].append(entry)
                arrays.append(copy)
        if n and share:
            choices = [(square_masks[0], None)]
            if square_masks[0] != square_masks[1]:
                choices = [(square_masks[0], True), (square_masks[1], False)]
            for m, flag in choices:
                for s, copy in enumerate(tails[m]):
                    if all(copy is not x for x in arrays):
                        arrays.append(copy)
                    at = [copy is x for x in arrays].index(True)
                    for p in range(4):
                        entries[SWAPPED[p] if s % 2 else p].append((at, p, early, share, s, flag))
        parts += [(square_masks, p, entries[p]) for p in range(4)]
    statics = (plan, parts, len(arrays), rows, cols, col_tiles, part, chunk)
    scratch = [
        pltpu.VMEM((supers, slots * TILE, width), jnp.float32),
        pltpu.VMEM((supers, row_tiles * TILE, width), jnp.float32),
        pltpu.VMEM((DEPTH, TILE, unit), jnp.float32),
        pltpu.VMEM((width, width), jnp.float32),
        pltpu.VMEM((packed, width // 2), jnp.float32),
        pltpu.SemaphoreType.DMA((supers * rows,)),
        pltpu.SemaphoreType.DMA((DEPTH,)),
        pltpu.SemaphoreType.DMA((supers * grains,)),
    ]
    call = pl.pallas_call(
        functools.partial(product_kernel, statics),
        out_shape=tuple(finals),
        in_specs=[smem] * 3 + [anywhere] * (2 + len(arrays)),
        out_specs=(anywhere,) * cols + (pl.BlockSpec(memory_space=pltpu.VMEM),) * (2 * cols),
        scratch_shapes=scratch,
        compiler_params=pltpu.CompilerParams(vmem_limit_bytes=66060288),
        name="listed_products",
    )
    carried = call(spot, tile_lists, lists, ancestor, panels, *arrays)
    product, corner = carried[:cols], carried[cols:]

    low, high = corner[0], corner[1]
    for m in sides:
        high = high + wires.sibling(corner[2 * m + 1], m)
    high = wires.first(high)
    for m in sides:
        low = low + wires.sibling(corner[2 * m], m)
    sums = low + high
    sums = sums[0] + wires.second(sums[1])
    for m in masks:
        if m & (m - 1) == 0:
            sums = sums + wires.square(sums, m)
    both = jnp.stack([sums, wires.second(sums)])
    others = wires.first(both)
    full = jnp.stack([both[0], others[0], both[1], others[1]])
    parts = [full] + [wires.sibling(full, s) for s in sides]
    moved = [wires.sibling(product[s], s) for s in sides]
    block = product[0]
    for x in moved:
        block = block + x
    first_row = r * ancestor.shape[0] + c * keep
    own_rows = first_row + jnp.arange(keep, dtype=jnp.int32)
    row_listed = jnp.any((own_rows // TILE)[None, :, None] == tile_lists[:, None, :], axis=2)
    block = jnp.where(row_listed[:, :, None], -block, 0.0)
    vmem = pl.BlockSpec(memory_space=pltpu.VMEM)
    diag = pl.pallas_call(
        functools.partial(corner_kernel, cols, chunk),
        out_shape=jax.ShapeDtypeStruct(diag_inverse.shape, jnp.float32),
        in_specs=[smem] + [vmem] * (1 + cols),
        out_specs=vmem,
        scratch_shapes=[pltpu.VMEM((packed, width // 2), jnp.float32)],
        name="corner_blocks",
    )(spot, diag_inverse, *parts)
    return block, diag


def solution(mesh):
    in_specs = (P("row", "col"), P(None, "row", None), P(), P())
    out_specs = (P(None, ("row", "col"), None), P())
    return jax.shard_map(local, mesh=mesh, in_specs=in_specs, out_specs=out_specs, check_vma=False)
```

```python
import functools

import jax
import jax.numpy as jnp
from jax import lax
from jax.experimental import pallas as pl
from jax.experimental.pallas import tpu as pltpu
from jax.sharding import PartitionSpec as P


AXES = ("row", "col")
TILE = 256
DEPTH = 12
TOGETHER = 4
SHARE = 24

SWAPPED = (0, 2, 1, 3)


def relative(place, odd):
    return jnp.where(odd, SWAPPED[place], place)


class Wires:
    def __init__(self, rows, cols):
        self.rows, self.cols = rows, cols

    def pairs(self, row_mask, col_mask=0, squares=None):
        pick = row_mask if callable(row_mask) else lambda c: row_mask
        return [
            (r * self.cols + c, (r ^ pick(c)) * self.cols + (c ^ col_mask))
            for r in range(self.rows)
            for c in range(self.cols)
            if squares is None or r // 4 in squares
        ]

    def first(self, x):
        return lax.ppermute(x, AXES, self.pairs(lambda c: 1 + c % 2))

    def second(self, x):
        return lax.ppermute(x, AXES, self.pairs(lambda c: 2 - c % 2))

    def square(self, x, mask, squares=None):
        return lax.ppermute(x, AXES, self.pairs(mask, squares=squares))

    def sibling(self, x, mask):
        return lax.ppermute(x, AXES, self.pairs(0, mask))


def over(x, d):
    return x >> (d.bit_length() - 1) if d & (d - 1) == 0 else x // d


def rest(x, d):
    return x & (d - 1) if d & (d - 1) == 0 else x % d


def split(x):
    high = x.astype(jnp.bfloat16)
    low = (x - high.astype(jnp.float32)).astype(jnp.bfloat16)
    return high, low


def left_of(x):
    high, low = split(x)
    return jnp.concatenate([low, high, high], axis=1)


def right_of(x):
    high, low = split(x)
    return jnp.concatenate([high, low, high], axis=0)


def dot(left, right):
    return jnp.dot(left, right, preferred_element_type=jnp.float32)


class Plan:
    def __init__(self, supers, rows, row_tiles):
        self.most = supers * rows
        self.counts = 0
        self.head = 2
        self.rows = self.head + supers + 1
        self.slots = self.rows + supers * row_tiles
        self.wanted = self.slots + supers * row_tiles
        self.only = self.wanted + self.most
        self.works = self.only + self.most
        self.size = self.works + self.most * row_tiles + TOGETHER


def square_base(r, masks):
    square = over(r, 4)
    inner = (square == 1) | (square == 2)
    return (r ^ jnp.where(inner, masks[0], masks[1])) & ~3, inner


def plan_kernel(plan, squares, rows, unit, row_tiles, col_tiles, spot_ref, list_ref, out):
    r, c = spot_ref[0], spot_ref[1]
    supers, slots = list_ref.shape

    def rows_of(n, count):
        k, s = over(n, slots), rest(n, slots)
        t = list_ref[k, s]
        take = over(t, row_tiles) == r

        @pl.when(s == 0)
        def _():
            out[plan.head + k] = count

        @pl.when(take)
        def _():
            out[plan.rows + count] = k * row_tiles + rest(t, row_tiles)
            out[plan.slots + count] = s

        return count + take.astype(jnp.int32)

    out[plan.head + supers] = lax.fori_loop(0, supers * slots, rows_of, jnp.int32(0))

    odd = (c % 2) == 1
    works, only = jnp.int32(0), jnp.int32(0)
    for masks in squares:
        base, _ = square_base(r, masks)
        for place in range(4):
            source = base + ((r & 3) ^ relative(place, odd))

            def each(k, counts, source=source):
                works, only = counts
                n = k * rows + source
                t = list_ref[k, over(source * unit, TILE)]
                low, high = out[plan.head + k], out[plan.head + k + 1]
                here = (over(t, col_tiles) == c) & (high > low)
                near = over(t, row_tiles) == r
                lone = near & jnp.logical_not(here)
                out[plan.wanted + n] = (here | near).astype(jnp.int32)

                @pl.when(lone)
                def _():
                    out[plan.only + only] = n

                def append(j, works):
                    out[plan.works + works] = n * row_tiles + rest(out[plan.rows + j], row_tiles)
                    return works + 1

                works = lax.fori_loop(low, jnp.where(here, high, low), append, works)
                return works, only + lone.astype(jnp.int32)

            works, only = lax.fori_loop(0, supers, each, (works, only))
    for extra in range(TOGETHER - 1):
        out[plan.works + works + extra] = out[plan.works + jnp.maximum(works - 1, 0)]
    out[plan.counts] = works
    out[plan.counts + 1] = only


def product_kernel(statics, spot_ref, list_ref, plan_ref, ancestor, panels, *refs):
    (plan, parts, n_pieces, rows, cols, col_tiles, part, chunk) = statics
    supers, unit, width = panels.shape
    row_tiles = ancestor.shape[0] // TILE
    keep = ancestor.shape[0] // cols
    half = width // 2
    pieces, outs = refs[:n_pieces], refs[n_pieces : n_pieces + 5 * cols]
    (panel, total, blocks, corner, pack, sem_p, sem_a, sem_o) = refs[
        n_pieces + 5 * cols :
    ]
    r, c = spot_ref[0], spot_ref[1]
    odd = (c % 2) == 1
    n_rows, n_works = plan_ref[plan.head + supers], plan_ref[plan.counts]

    def loop(count, body):
        def step(n, _):
            body(n)
            return 0

        lax.fori_loop(0, count, step, 0)

    def tile_rows(i):
        return pl.ds(pl.multiple_of(i * TILE, TILE), TILE)

    def work_of(w):
        code = plan_ref[plan.works + w]
        return over(code, row_tiles), rest(code, row_tiles)

    def fetch(w):
        n, i = work_of(w)
        k, source = over(n, rows), rest(n, rows)
        t = list_ref[k, over(source * unit, TILE)]
        col = pl.multiple_of((t - c * col_tiles) * TILE + rest(source * unit, TILE), min(unit, TILE))
        slot = lax.rem(w, DEPTH)
        return pltpu.make_async_copy(
            ancestor.at[tile_rows(i), pl.ds(col, unit)], blocks.at[slot], sem_a.at[slot]
        )

    for w in range(DEPTH):
        pl.when(w < n_works)(lambda w=w: fetch(w).start())

    for masks, place, entries in parts:
        base, inner = square_base(r, masks)
        source = base + ((r & 3) ^ relative(place, odd))


        def start_panels(k, entries=entries, inner=inner, source=source):
            n = k * rows + source

            @pl.when(plan_ref[plan.wanted + n] != 0)
            def _():
                for piece, index, offset, size, side, where_inner in entries:

                    def go(piece=piece, index=index, offset=offset, size=size, side=side):
                        start = source * unit + offset
                        if side is not None:
                            start = start + (c ^ side) * part
                        ref = panels if piece is None else pieces[piece]
                        pltpu.make_async_copy(
                            ref.at[k] if index is None else ref.at[index, k],
                            panel.at[k, pl.ds(pl.multiple_of(start, 8), size), :],
                            sem_p.at[n],
                        ).start()

                    if where_inner is None:
                        go()
                    else:
                        pl.when(inner == where_inner)(go)

        loop(supers, start_panels)

    def unit_of(n):
        return panel.at[over(n, rows), pl.ds(pl.multiple_of(rest(n, rows) * unit, unit), unit), :]

    def wait_panel(n):
        pltpu.make_async_copy(panels.at[0], unit_of(n), sem_p.at[n]).wait()

    def clear(n):
        code = plan_ref[plan.rows + n]
        k, i = over(code, row_tiles), rest(code, row_tiles)
        total[k, tile_rows(i), :] = jnp.zeros((TILE, width), jnp.float32)

    loop(n_rows, clear)

    grain = min(TILE, keep)
    grains = TILE // grain

    def result(k, row, ref, sem, go):
        target_rows = pl.ds(pl.multiple_of(rest(row, keep), grain), grain)
        for mask in range(cols):

            @pl.when(over(row, keep) ^ c == mask)
            def _():
                copy = pltpu.make_async_copy(ref, outs[mask].at[k, target_rows, :], sem)
                copy.start() if go else copy.wait()

    def listed(n, go):
        code = plan_ref[plan.rows + n]
        k, i = over(code, row_tiles), rest(code, row_tiles)
        for g in range(grains):
            row = i * TILE + g * grain
            ref = total.at[k, pl.ds(pl.multiple_of(row, grain), grain), :]
            result(k, row, ref, sem_o.at[code * grains + g], go)

    def multiply(v, before):
        first = v * TOGETHER
        sums, spots = [], []
        for w in range(TOGETHER):
            n, _ = work_of(first + w)
            pl.when(before != n)(lambda n=n: wait_panel(n))
            pl.when(first + w < n_works)(lambda w=w: fetch(first + w).wait())
            before = n
        for w in range(TOGETHER):
            n, i = work_of(first + w)
            block = blocks[lax.rem(first + w, DEPTH)]
            if w:
                block = jnp.where(first + w < n_works, block, 0.0)
            sums.append(dot(left_of(block), right_of(unit_of(n)[...])))
            spots.append((over(n, rows), i))
        for (k, i), x in zip(spots, sums):
            total[k, tile_rows(i), :] += x
        for w in range(TOGETHER):
            later = first + w + DEPTH
            pl.when(later < n_works)(lambda later=later: fetch(later).start())
        return before

    lax.fori_loop(0, (n_works + TOGETHER - 1) // TOGETHER, multiply, jnp.int32(-1))
    loop(n_rows, lambda n: listed(n, True))
    loop(plan_ref[plan.counts + 1], lambda m: wait_panel(plan_ref[plan.only + m]))

    def corners(k, _):
        corner[...] = jnp.zeros_like(corner)

        def product(n):
            here = tile_rows(rest(plan_ref[plan.rows + n], row_tiles))
            near = panel[k, tile_rows(plan_ref[plan.slots + n]), :]
            return dot(left_of(near.T), right_of(total[k, here, :]))

        low, high = plan_ref[plan.head + k], plan_ref[plan.head + k + 1]

        def two(n, _):
            corner[...] += product(low + 2 * n) + product(low + 2 * n + 1)
            return 0

        lax.fori_loop(0, (high - low) >> 1, two, 0)

        @pl.when(((high - low) & 1) == 1)
        def _():
            corner[...] += product(high - 1)

        start = pl.multiple_of(k * 3 * half, half)
        pack[pl.ds(start, half), :] = corner[:half, :half]
        pack[pl.ds(start + half, half), :] = corner[:half, half:]
        pack[pl.ds(start + 2 * half, half), :] = corner[half:, half:]
        return 0

    lax.fori_loop(0, supers, corners, 0)
    for mask in range(cols):
        for place in range(4):
            owner = c ^ mask
            spot = (r & 3) ^ relative(place, (owner % 2) == 1)
            rows_at = pl.ds(pl.multiple_of((owner * 4 + spot) * chunk, 8), chunk)
            outs[cols + 4 * mask + place][...] = pack[rows_at, :]
    loop(n_rows, lambda n: listed(n, False))


def corner_kernel(cols, chunk, spot_ref, inverse, *refs):
    parts, out, pack = refs[: 4 * cols], refs[4 * cols], refs[4 * cols + 1]
    r, c = spot_ref[0], spot_ref[1]
    for mask in range(cols):
        owner = c ^ mask
        for place in range(4):
            spot = (r & 3) ^ relative(place, (owner % 2) == 1)
            start = pl.multiple_of((owner * 4 + spot) * chunk, 8)
            pack[pl.ds(start, chunk), :] = parts[4 * mask + place][...]
    half = inverse.shape[1] // 2
    for k in range(inverse.shape[0]):
        base = k * 3 * half
        cross = pack[base + half : base + 2 * half, :]
        out[k, :half, :half] = inverse[k, :half, :half] + pack[base : base + half, :]
        out[k, :half, half:] = inverse[k, :half, half:] + cross
        out[k, half:, :half] = inverse[k, half:, :half] + cross.T
        out[k, half:, half:] = inverse[k, half:, half:] + pack[base + 2 * half : base + 3 * half, :]


def local(ancestor, panels, tile_lists, diag_inverse):
    rows, cols = lax.axis_size("row"), lax.axis_size("col")
    r, c = lax.axis_index("row"), lax.axis_index("col")
    spot = jnp.stack([r, c]).astype(jnp.int32)
    wires = Wires(rows, cols)
    supers, unit, width = panels.shape
    slots = tile_lists.shape[1]
    row_tiles, col_tiles = ancestor.shape[0] // TILE, ancestor.shape[1] // TILE
    part = unit // cols
    share = part * SHARE // 128 // 8 * 8
    early = part - share
    masks = [4 * m for m in range(1, rows // 4)]

    mine = lax.dynamic_slice_in_dim(panels, c * part, part, 1)
    front = lax.dynamic_slice_in_dim(panels, c * part, early, 1)

    def around(held):
        near = wires.first(held)
        return [held, near, wires.second(held), wires.second(near)]

    own = around(mine)

    if rows == 16:
        inner = (r // 4 == 1) | (r // 4 == 2)
        z1 = wires.square(front, 4)
        z2 = wires.square(front, 12, (1, 2))
        z3 = wires.square(z1, 12, (1, 2))
        z4 = wires.square(z2, 4, (1, 2))
        z5 = wires.square(z3, 4, (1, 2))
        far = [((4, 4), z1), ((12, 8), jnp.where(inner, z2, z4)), ((8, 12), jnp.where(inner, z3, z5))]
    else:
        far = [((m, m), wires.square(front, m)) for m in masks]
    ends = jnp.stack([x[:, early:] for x in own])
    tails = {m: wires.square(ends, m) for m in masks}
    sides = range(1, cols)
    tails = {m: [x] + [wires.sibling(x, s) for s in sides] for m, x in tails.items()}

    smem = pl.BlockSpec(memory_space=pltpu.SMEM)
    anywhere = pl.BlockSpec(memory_space=pltpu.HBM)
    keep = ancestor.shape[0] // cols
    packed = supers * 3 * (width // 2)
    chunk = packed // (4 * cols)
    grains = row_tiles * (TILE // min(TILE, keep))
    finals = [jax.ShapeDtypeStruct((supers, keep, width), jnp.float32)] * cols
    finals += [jax.ShapeDtypeStruct((chunk, width // 2), jnp.float32)] * (4 * cols)
    items = [((0, 0), own)] + [(m, around(held)) for m, held in far]
    plan = Plan(supers, rows, row_tiles)
    planner = pl.pallas_call(
        functools.partial(plan_kernel, plan, [m for m, _ in items], rows, unit, row_tiles, col_tiles),
        out_shape=jax.ShapeDtypeStruct((plan.size,), jnp.int32),
        in_specs=[smem, smem],
        out_specs=smem,
        name="plan",
    )
    lists = planner(spot, tile_lists)
    arrays, parts = [], []
    for n, (square_masks, groups) in enumerate(items):
        entries = [[] for _ in range(4)]
        for p, array in enumerate(groups):
            if n == 0 and p == 0:
                entries[0].append((None, None, 0, unit, None, None))
                continue
            copies = [array] + [wires.sibling(array, s) for s in sides]
            for s, copy in enumerate(copies):
                entry = (len(arrays), None, 0, array.shape[1], s, None)
                entries[SWAPPED[p] if s % 2 else p].append(entry)
                arrays.append(copy)
        if n and share:
            choices = [(square_masks[0], None)]
            if square_masks[0] != square_masks[1]:
                choices = [(square_masks[0], True), (square_masks[1], False)]
            for m, flag in choices:
                for s, copy in enumerate(tails[m]):
                    if all(copy is not x for x in arrays):
                        arrays.append(copy)
                    at = [copy is x for x in arrays].index(True)
                    for p in range(4):
                        entries[SWAPPED[p] if s % 2 else p].append((at, p, early, share, s, flag))
        parts += [(square_masks, p, entries[p]) for p in range(4)]
    statics = (plan, parts, len(arrays), rows, cols, col_tiles, part, chunk)
    scratch = [
        pltpu.VMEM((supers, slots * TILE, width), jnp.float32),
        pltpu.VMEM((supers, row_tiles * TILE, width), jnp.float32),
        pltpu.VMEM((DEPTH, TILE, unit), jnp.float32),
        pltpu.VMEM((width, width), jnp.float32),
        pltpu.VMEM((packed, width // 2), jnp.float32),
        pltpu.SemaphoreType.DMA((supers * rows,)),
        pltpu.SemaphoreType.DMA((DEPTH,)),
        pltpu.SemaphoreType.DMA((supers * grains,)),
    ]
    call = pl.pallas_call(
        functools.partial(product_kernel, statics),
        out_shape=tuple(finals),
        in_specs=[smem] * 3 + [anywhere] * (2 + len(arrays)),
        out_specs=(anywhere,) * cols + (pl.BlockSpec(memory_space=pltpu.VMEM),) * (4 * cols),
        scratch_shapes=scratch,
        compiler_params=pltpu.CompilerParams(vmem_limit_bytes=66060288),
        name="listed_products",
    )
    carried = call(spot, tile_lists, lists, ancestor, panels, *arrays)
    product, corner = carried[:cols], carried[cols:]

    sums = list(corner[:4])
    for p in (3, 1, 2, 0):
        for m in sides:
            sums[p] = sums[p] + wires.sibling(corner[4 * m + p], m)
    late = wires.first(sums[3])
    near = wires.first(sums[1])
    late = wires.second(sums[2] + late)
    mine = (sums[0] + near) + late
    for m in masks:
        if m & (m - 1) == 0:
            mine = mine + wires.square(mine, m)
    across = wires.second(mine)
    beside = wires.first(mine)
    corner_own = [mine, beside, across, wires.first(across)]
    parts = list(corner_own)
    for m in sides:
        parts += [wires.sibling(x, m) for x in corner_own]
    moved = [wires.sibling(product[s], s) for s in sides]
    block = product[0]
    for x in moved:
        block = block + x
    first_row = r * ancestor.shape[0] + c * keep
    own_rows = first_row + jnp.arange(keep, dtype=jnp.int32)
    row_listed = jnp.any((own_rows // TILE)[None, :, None] == tile_lists[:, None, :], axis=2)
    block = jnp.where(row_listed[:, :, None], -block, 0.0)
    vmem = pl.BlockSpec(memory_space=pltpu.VMEM)
    diag = pl.pallas_call(
        functools.partial(corner_kernel, cols, chunk),
        out_shape=jax.ShapeDtypeStruct(diag_inverse.shape, jnp.float32),
        in_specs=[smem] + [vmem] * (1 + 4 * cols),
        out_specs=vmem,
        scratch_shapes=[pltpu.VMEM((packed, width // 2), jnp.float32)],
        name="corner_blocks",
    )(spot, diag_inverse, *parts)
    return block, diag


def solution(mesh):
    in_specs = (P("row", "col"), P(None, "row", None), P(), P())
    out_specs = (P(None, ("row", "col"), None), P())
    return jax.shard_map(local, mesh=mesh, in_specs=in_specs, out_specs=out_specs, check_vma=False)
```

```python
import functools

import jax
import jax.numpy as jnp
from jax import lax
from jax.experimental import pallas as pl
from jax.experimental.pallas import tpu as pltpu
from jax.sharding import PartitionSpec as P


AXES = ("row", "col")
TILE = 256
DEPTH = 12
TOGETHER = 4
SHARE = 24

SWAPPED = (0, 2, 1, 3)


def relative(place, odd):
    return jnp.where(odd, SWAPPED[place], place)


class Wires:
    def __init__(self, rows, cols):
        self.rows, self.cols = rows, cols

    def pairs(self, row_mask, col_mask=0, squares=None):
        pick = row_mask if callable(row_mask) else lambda c: row_mask
        return [
            (r * self.cols + c, (r ^ pick(c)) * self.cols + (c ^ col_mask))
            for r in range(self.rows)
            for c in range(self.cols)
            if squares is None or r // 4 in squares
        ]

    def first(self, x):
        return lax.ppermute(x, AXES, self.pairs(lambda c: 1 + c % 2))

    def second(self, x):
        return lax.ppermute(x, AXES, self.pairs(lambda c: 2 - c % 2))

    def square(self, x, mask, squares=None):
        return lax.ppermute(x, AXES, self.pairs(mask, squares=squares))

    def sibling(self, x, mask):
        return lax.ppermute(x, AXES, self.pairs(0, mask))


def over(x, d):
    return x >> (d.bit_length() - 1) if d & (d - 1) == 0 else x // d


def rest(x, d):
    return x & (d - 1) if d & (d - 1) == 0 else x % d


def split(x):
    high = x.astype(jnp.bfloat16)
    low = (x - high.astype(jnp.float32)).astype(jnp.bfloat16)
    return high, low


def left_of(x):
    high, low = split(x)
    return jnp.concatenate([low, high, high], axis=1)


def right_of(x):
    high, low = split(x)
    return jnp.concatenate([high, low, high], axis=0)


def dot(left, right):
    return jnp.dot(left, right, preferred_element_type=jnp.float32)


class Plan:
    def __init__(self, supers, rows, row_tiles):
        self.most = supers * rows
        self.counts = 0
        self.head = 2
        self.rows = self.head + supers + 1
        self.slots = self.rows + supers * row_tiles
        self.wanted = self.slots + supers * row_tiles
        self.only = self.wanted + self.most
        self.works = self.only + self.most
        self.size = self.works + self.most * row_tiles + TOGETHER


def square_base(r, masks):
    square = over(r, 4)
    inner = (square == 1) | (square == 2)
    return (r ^ jnp.where(inner, masks[0], masks[1])) & ~3, inner


def plan_kernel(plan, squares, rows, unit, row_tiles, col_tiles, spot_ref, list_ref, out):
    r, c = spot_ref[0], spot_ref[1]
    supers, slots = list_ref.shape

    def rows_of(n, count):
        k, s = over(n, slots), rest(n, slots)
        t = list_ref[k, s]
        take = over(t, row_tiles) == r

        @pl.when(s == 0)
        def _():
            out[plan.head + k] = count

        @pl.when(take)
        def _():
            out[plan.rows + count] = k * row_tiles + rest(t, row_tiles)
            out[plan.slots + count] = s

        return count + take.astype(jnp.int32)

    out[plan.head + supers] = lax.fori_loop(0, supers * slots, rows_of, jnp.int32(0))

    odd = (c % 2) == 1
    works, only = jnp.int32(0), jnp.int32(0)
    for masks in squares:
        base, _ = square_base(r, masks)
        for place in range(4):
            source = base + ((r & 3) ^ relative(place, odd))

            def each(k, counts, source=source):
                works, only = counts
                n = k * rows + source
                t = list_ref[k, over(source * unit, TILE)]
                low, high = out[plan.head + k], out[plan.head + k + 1]
                here = (over(t, col_tiles) == c) & (high > low)
                near = over(t, row_tiles) == r
                lone = near & jnp.logical_not(here)
                out[plan.wanted + n] = (here | near).astype(jnp.int32)

                @pl.when(lone)
                def _():
                    out[plan.only + only] = n

                def append(j, works):
                    out[plan.works + works] = n * row_tiles + rest(out[plan.rows + j], row_tiles)
                    return works + 1

                works = lax.fori_loop(low, jnp.where(here, high, low), append, works)
                return works, only + lone.astype(jnp.int32)

            works, only = lax.fori_loop(0, supers, each, (works, only))
    for extra in range(TOGETHER - 1):
        out[plan.works + works + extra] = out[plan.works + jnp.maximum(works - 1, 0)]
    out[plan.counts] = works
    out[plan.counts + 1] = only


def product_kernel(statics, spot_ref, list_ref, plan_ref, ancestor, panels, *refs):
    (plan, parts, n_pieces, rows, cols, col_tiles, part, chunk) = statics
    supers, unit, width = panels.shape
    row_tiles = ancestor.shape[0] // TILE
    keep = ancestor.shape[0] // cols
    half = width // 2
    pieces, outs = refs[:n_pieces], refs[n_pieces : n_pieces + 5 * cols]
    (panel, total, blocks, corner, pack, sem_p, sem_a, sem_o) = refs[
        n_pieces + 5 * cols :
    ]
    r, c = spot_ref[0], spot_ref[1]
    odd = (c % 2) == 1
    n_rows, n_works = plan_ref[plan.head + supers], plan_ref[plan.counts]

    def loop(count, body):
        def step(n, _):
            body(n)
            return 0

        lax.fori_loop(0, count, step, 0)

    def tile_rows(i):
        return pl.ds(pl.multiple_of(i * TILE, TILE), TILE)

    def work_of(w):
        code = plan_ref[plan.works + w]
        return over(code, row_tiles), rest(code, row_tiles)

    def fetch(w):
        n, i = work_of(w)
        k, source = over(n, rows), rest(n, rows)
        t = list_ref[k, over(source * unit, TILE)]
        col = pl.multiple_of((t - c * col_tiles) * TILE + rest(source * unit, TILE), min(unit, TILE))
        slot = lax.rem(w, DEPTH)
        return pltpu.make_async_copy(
            ancestor.at[tile_rows(i), pl.ds(col, unit)], blocks.at[slot], sem_a.at[slot]
        )

    for w in range(DEPTH):
        pl.when(w < n_works)(lambda w=w: fetch(w).start())

    for masks, place, entries in parts:
        base, inner = square_base(r, masks)
        source = base + ((r & 3) ^ relative(place, odd))


        def start_panels(k, entries=entries, inner=inner, source=source):
            n = k * rows + source

            @pl.when(plan_ref[plan.wanted + n] != 0)
            def _():
                for piece, index, offset, size, side, where_inner in entries:

                    def go(piece=piece, index=index, offset=offset, size=size, side=side):
                        start = source * unit + offset
                        if side is not None:
                            start = start + (c ^ side) * part
                        ref = panels if piece is None else pieces[piece]
                        pltpu.make_async_copy(
                            ref.at[k] if index is None else ref.at[index, k],
                            panel.at[k, pl.ds(pl.multiple_of(start, 8), size), :],
                            sem_p.at[n],
                        ).start()

                    if where_inner is None:
                        go()
                    else:
                        pl.when(inner == where_inner)(go)

        loop(supers, start_panels)

    def unit_of(n):
        return panel.at[over(n, rows), pl.ds(pl.multiple_of(rest(n, rows) * unit, unit), unit), :]

    def wait_panel(n):
        pltpu.make_async_copy(panels.at[0], unit_of(n), sem_p.at[n]).wait()

    def clear(n):
        code = plan_ref[plan.rows + n]
        k, i = over(code, row_tiles), rest(code, row_tiles)
        total[k, tile_rows(i), :] = jnp.zeros((TILE, width), jnp.float32)

    loop(n_rows, clear)

    grain = min(TILE, keep)
    grains = TILE // grain

    def result(k, row, ref, sem, go):
        target_rows = pl.ds(pl.multiple_of(rest(row, keep), grain), grain)
        for mask in range(cols):

            @pl.when(over(row, keep) ^ c == mask)
            def _():
                copy = pltpu.make_async_copy(ref, outs[mask].at[k, target_rows, :], sem)
                copy.start() if go else copy.wait()

    def listed(n, go):
        code = plan_ref[plan.rows + n]
        k, i = over(code, row_tiles), rest(code, row_tiles)
        for g in range(grains):
            row = i * TILE + g * grain
            ref = total.at[k, pl.ds(pl.multiple_of(row, grain), grain), :]
            result(k, row, ref, sem_o.at[code * grains + g], go)

    def multiply(v, before):
        first = v * TOGETHER
        sums, spots = [], []
        for w in range(TOGETHER):
            n, _ = work_of(first + w)
            pl.when(before != n)(lambda n=n: wait_panel(n))
            pl.when(first + w < n_works)(lambda w=w: fetch(first + w).wait())
            before = n
        for w in range(TOGETHER):
            n, i = work_of(first + w)
            block = blocks[lax.rem(first + w, DEPTH)]
            if w:
                block = jnp.where(first + w < n_works, block, 0.0)
            sums.append(dot(left_of(block), right_of(unit_of(n)[...])))
            spots.append((over(n, rows), i))
        for (k, i), x in zip(spots, sums):
            total[k, tile_rows(i), :] += x
        for w in range(TOGETHER):
            later = first + w + DEPTH
            pl.when(later < n_works)(lambda later=later: fetch(later).start())
        return before

    lax.fori_loop(0, (n_works + TOGETHER - 1) // TOGETHER, multiply, jnp.int32(-1))
    loop(n_rows, lambda n: listed(n, True))
    loop(plan_ref[plan.counts + 1], lambda m: wait_panel(plan_ref[plan.only + m]))

    def corners(k, _):
        corner[...] = jnp.zeros_like(corner)

        def product(n):
            here = tile_rows(rest(plan_ref[plan.rows + n], row_tiles))
            near = panel[k, tile_rows(plan_ref[plan.slots + n]), :]
            return dot(left_of(near.T), right_of(total[k, here, :]))

        low, high = plan_ref[plan.head + k], plan_ref[plan.head + k + 1]

        def two(n, _):
            corner[...] += product(low + 2 * n) + product(low + 2 * n + 1)
            return 0

        lax.fori_loop(0, (high - low) >> 1, two, 0)

        @pl.when(((high - low) & 1) == 1)
        def _():
            corner[...] += product(high - 1)

        start = pl.multiple_of(k * 3 * half, half)
        pack[pl.ds(start, half), :] = corner[:half, :half]
        pack[pl.ds(start + half, half), :] = corner[:half, half:]
        pack[pl.ds(start + 2 * half, half), :] = corner[half:, half:]
        return 0

    lax.fori_loop(0, supers, corners, 0)
    for mask in range(cols):
        for place in range(4):
            owner = c ^ mask
            spot = (r & 3) ^ relative(place, (owner % 2) == 1)
            rows_at = pl.ds(pl.multiple_of((owner * 4 + spot) * chunk, 8), chunk)
            outs[cols + 4 * mask + place][...] = pack[rows_at, :]
    loop(n_rows, lambda n: listed(n, False))


def corner_kernel(cols, chunk, spot_ref, inverse, *refs):
    parts, out, pack = refs[: 4 * cols], refs[4 * cols], refs[4 * cols + 1]
    r, c = spot_ref[0], spot_ref[1]
    for mask in range(cols):
        owner = c ^ mask
        for place in range(4):
            spot = (r & 3) ^ relative(place, (owner % 2) == 1)
            start = pl.multiple_of((owner * 4 + spot) * chunk, 8)
            pack[pl.ds(start, chunk), :] = parts[4 * mask + place][...]
    half = inverse.shape[1] // 2
    for k in range(inverse.shape[0]):
        base = k * 3 * half
        cross = pack[base + half : base + 2 * half, :]
        out[k, :half, :half] = inverse[k, :half, :half] + pack[base : base + half, :]
        out[k, :half, half:] = inverse[k, :half, half:] + cross
        out[k, half:, :half] = inverse[k, half:, :half] + cross.T
        out[k, half:, half:] = inverse[k, half:, half:] + pack[base + 2 * half : base + 3 * half, :]


def local(ancestor, panels, tile_lists, diag_inverse):
    rows, cols = lax.axis_size("row"), lax.axis_size("col")
    r, c = lax.axis_index("row"), lax.axis_index("col")
    spot = jnp.stack([r, c]).astype(jnp.int32)
    wires = Wires(rows, cols)
    supers, unit, width = panels.shape
    slots = tile_lists.shape[1]
    row_tiles, col_tiles = ancestor.shape[0] // TILE, ancestor.shape[1] // TILE
    part = unit // cols
    share = part * SHARE // 128 // 8 * 8
    early = part - share
    masks = [4 * m for m in range(1, rows // 4)]

    mine = lax.dynamic_slice_in_dim(panels, c * part, part, 1)
    front = lax.dynamic_slice_in_dim(panels, c * part, early, 1)

    def around(held):
        near = wires.first(held)
        return [held, near, wires.second(held), wires.second(near)]

    own = around(mine)

    if rows == 16:
        inner = (r // 4 == 1) | (r // 4 == 2)
        z1 = wires.square(front, 4)
        z2 = wires.square(front, 12, (1, 2))
        z3 = wires.square(z1, 12, (1, 2))
        z4 = wires.square(z2, 4, (1, 2))
        z5 = wires.square(z3, 4, (1, 2))
        far = [((4, 4), z1), ((12, 8), jnp.where(inner, z2, z4)), ((8, 12), jnp.where(inner, z3, z5))]
    else:
        far = [((m, m), wires.square(front, m)) for m in masks]
    ends = jnp.stack([x[:, early:] for x in own])
    tails = {m: wires.square(ends, m) for m in masks}
    sides = range(1, cols)
    tails = {m: [x] + [wires.sibling(x, s) for s in sides] for m, x in tails.items()}

    smem = pl.BlockSpec(memory_space=pltpu.SMEM)
    anywhere = pl.BlockSpec(memory_space=pltpu.HBM)
    keep = ancestor.shape[0] // cols
    packed = supers * 3 * (width // 2)
    chunk = packed // (4 * cols)
    grains = row_tiles * (TILE // min(TILE, keep))
    finals = [jax.ShapeDtypeStruct((supers, keep, width), jnp.float32)] * cols
    finals += [jax.ShapeDtypeStruct((chunk, width // 2), jnp.float32)] * (4 * cols)
    items = [((0, 0), own)] + [(m, around(held)) for m, held in far]
    plan = Plan(supers, rows, row_tiles)
    planner = pl.pallas_call(
        functools.partial(plan_kernel, plan, [m for m, _ in items], rows, unit, row_tiles, col_tiles),
        out_shape=jax.ShapeDtypeStruct((plan.size,), jnp.int32),
        in_specs=[smem, smem],
        out_specs=smem,
        name="plan",
    )
    lists = planner(spot, tile_lists)
    arrays, parts = [], []
    for n, (square_masks, groups) in enumerate(items):
        entries = [[] for _ in range(4)]
        for p, array in enumerate(groups):
            if n == 0 and p == 0:
                entries[0].append((None, None, 0, unit, None, None))
                continue
            copies = [array] + [wires.sibling(array, s) for s in sides]
            for s, copy in enumerate(copies):
                entry = (len(arrays), None, 0, array.shape[1], s, None)
                entries[SWAPPED[p] if s % 2 else p].append(entry)
                arrays.append(copy)
        if n and share:
            choices = [(square_masks[0], None)]
            if square_masks[0] != square_masks[1]:
                choices = [(square_masks[0], True), (square_masks[1], False)]
            for m, flag in choices:
                for s, copy in enumerate(tails[m]):
                    if all(copy is not x for x in arrays):
                        arrays.append(copy)
                    at = [copy is x for x in arrays].index(True)
                    for p in range(4):
                        entries[SWAPPED[p] if s % 2 else p].append((at, p, early, share, s, flag))
        parts += [(square_masks, p, entries[p]) for p in range(4)]
    statics = (plan, parts, len(arrays), rows, cols, col_tiles, part, chunk)
    scratch = [
        pltpu.VMEM((supers, slots * TILE, width), jnp.float32),
        pltpu.VMEM((supers, row_tiles * TILE, width), jnp.float32),
        pltpu.VMEM((DEPTH, TILE, unit), jnp.float32),
        pltpu.VMEM((width, width), jnp.float32),
        pltpu.VMEM((packed, width // 2), jnp.float32),
        pltpu.SemaphoreType.DMA((supers * rows,)),
        pltpu.SemaphoreType.DMA((DEPTH,)),
        pltpu.SemaphoreType.DMA((supers * grains,)),
    ]
    call = pl.pallas_call(
        functools.partial(product_kernel, statics),
        out_shape=tuple(finals),
        in_specs=[smem] * 3 + [anywhere] * (2 + len(arrays)),
        out_specs=(anywhere,) * cols + (pl.BlockSpec(memory_space=pltpu.VMEM),) * (4 * cols),
        scratch_shapes=scratch,
        compiler_params=pltpu.CompilerParams(vmem_limit_bytes=66060288),
        name="listed_products",
    )
    carried = call(spot, tile_lists, lists, ancestor, panels, *arrays)
    product, corner = carried[:cols], carried[cols:]

    sums = list(corner[:4])
    for p in (3, 1, 2, 0):
        for m in sides:
            sums[p] = sums[p] + wires.sibling(corner[4 * m + p], m)
    cross = wires.square(sums[3], 3)
    near = wires.first(sums[1])
    next_near = wires.second(sums[2])
    mine = (sums[0] + near) + (next_near + cross)
    for m in masks:
        if m & (m - 1) == 0:
            mine = mine + wires.square(mine, m)
    corner_own = [mine, wires.first(mine), wires.second(mine)]
    corner_own += [wires.square(mine, 3)]
    parts = list(corner_own)
    for m in sides:
        parts += [wires.sibling(x, m) for x in corner_own]
    moved = [wires.sibling(product[s], s) for s in sides]
    block = product[0]
    for x in moved:
        block = block + x
    first_row = r * ancestor.shape[0] + c * keep
    own_rows = first_row + jnp.arange(keep, dtype=jnp.int32)
    row_listed = jnp.any((own_rows // TILE)[None, :, None] == tile_lists[:, None, :], axis=2)
    block = jnp.where(row_listed[:, :, None], -block, 0.0)
    vmem = pl.BlockSpec(memory_space=pltpu.VMEM)
    diag = pl.pallas_call(
        functools.partial(corner_kernel, cols, chunk),
        out_shape=jax.ShapeDtypeStruct(diag_inverse.shape, jnp.float32),
        in_specs=[smem] + [vmem] * (1 + 4 * cols),
        out_specs=vmem,
        scratch_shapes=[pltpu.VMEM((packed, width // 2), jnp.float32)],
        name="corner_blocks",
    )(spot, diag_inverse, *parts)
    return block, diag


def solution(mesh):
    in_specs = (P("row", "col"), P(None, "row", None), P(), P())
    out_specs = (P(None, ("row", "col"), None), P())
    return jax.shard_map(local, mesh=mesh, in_specs=in_specs, out_specs=out_specs, check_vma=False)
```
